32 devices in a mesh: row: 8 (over y, x, core), col: 4 (over z).
Axes of the slice: x: 2, y: 2, z: 4, core: 2. Of those that a mesh axis runs over, the one named last changes fastest.
Arguments:
- documents: float32 [6144, 768], P('row', 'col'), may hold values from -6 to 6
- projection: float32 [768, 768], P('col'), may hold values from -0.21875 to 0.21875
- landmarks: float32 [16384, 768], P('col', 'row'), may hold values from -6 to 6
- coefficients: float32 [16384, 128], P('col'), may hold values from -6 to 6
- inverse_tiles: float32 [16384, 16384], P('col', 'row'), may hold values from -0.046875 to 0.046875
- labels: int32 [6144, 128], P('row'), may hold values 0 or 1
Outputs:
- new_coefficients: float32 [16384, 128], P('col')
- residual: float32 [6144, 128], P('row')
The draws below stay inside these ranges and needn't reach their ends.
All inputs are finite; a program needn't handle non-finite values. No bound on the sum of `labels` on one device may be relied on, other than what follows from the above.
Results may differ from the reference program's by a relative error of at most 0.0001.
Values sent between devices are 32-bit elements; how exact they have to be, the bound alone decides.
A program may use at most 128 MiB of HBM per device.

```python
import jax
import jax.numpy as jnp
from jax import lax

D = 768
M = 16384
LABELS = 128
ITERS = 2
DOCS = 6144


def plant(array, key, smallest, largest):
    spot = [jax.random.randint(jax.random.fold_in(key, axis), (), 0, length) for axis, length in enumerate(array.shape)]
    main_axis = array.shape.index(max(array.shape))
    next_to = spot[:main_axis] + [(spot[main_axis] + 1) % array.shape[main_axis]] + spot[main_axis + 1:]
    return array.at[tuple(spot)].set(smallest).at[tuple(next_to)].set(largest)


def block_levels(key, shape, cuts, low, high):
    level, own = 1.0, jax.random.fold_in(key, 6)
    for axis_at, blocks in cuts:
        draws = jnp.exp(jax.random.uniform(jax.random.fold_in(own, axis_at), (blocks,), jnp.float32, low / len(cuts), high / len(cuts)))
        level = level * jnp.repeat(draws, shape[axis_at] // blocks).reshape([-1 if axis == axis_at else 1 for axis in range(len(shape))])
    return level


def normal_values(own_key, extent, width, bound, split=(), held_as=jnp.bfloat16):
    result = width * jax.random.normal(own_key, extent, jnp.float32)
    if split:
        result = result * block_levels(own_key, extent, split, -0.22, 0.18)
    return jnp.clip(result, -bound, bound).astype(held_as)


def setup_inputs(seed: int = 0) -> dict:
    key_of = jax.random.split(jax.random.key(seed), 7)
    return {
        "documents": normal_values(key_of[0], (DOCS, D), 1.0, 6.0, ((0, 8), (1, 4)), jnp.float32),
        "projection": normal_values(key_of[1], (D, D), D ** -0.5, 0.21875, ((0, 4),), jnp.float32),
        "landmarks": normal_values(key_of[2], (M, D), 1.0, 6.0, ((0, 4), (1, 8)), jnp.float32),
        "coefficients": normal_values(key_of[3], (M, LABELS), 1.0, 6.0, ((0, 4),), jnp.float32),
        "inverse_tiles": normal_values(key_of[4], (M, M), M ** -0.5, 0.046875, ((0, 4), (1, 8)), jnp.float32),
        "labels": plant((jax.random.randint(key_of[5], (DOCS, LABELS), 0, 3) < 1).astype(jnp.int32), jax.random.fold_in(key_of[5], 1), 0, 1),
    }


def reference(documents, projection, landmarks, coefficients, inverse_tiles, labels):
    highest = lax.Precision.HIGHEST
    proj = jnp.dot(documents, projection, precision=highest, preferred_element_type=jnp.float32)
    sq_doc = jnp.sum(proj * proj, axis=1)
    sq_land = jnp.sum(landmarks * landmarks, axis=1)
    inner = jnp.dot(proj, landmarks.T, precision=highest, preferred_element_type=jnp.float32)
    kernel = jnp.exp(-2.0 * (sq_doc[:, None] + sq_land[None, :] - 2.0 * inner) / D)
    step_size = 64.0 / DOCS
    current = coefficients
    target = labels.astype(jnp.float32)
    residual = jnp.zeros((DOCS, LABELS), jnp.float32)
    for iteration in range(ITERS):
        predicted = jnp.dot(kernel, current, precision=highest, preferred_element_type=jnp.float32)
        residual = jax.nn.sigmoid(predicted) - target
        gradient = jnp.dot(kernel.T, residual, precision=highest, preferred_element_type=jnp.float32)
        current = current - step_size * jnp.dot(inverse_tiles, gradient, precision=highest, preferred_element_type=jnp.float32)
    return current, residual
```

```python
import functools

import jax
import jax.numpy as jnp
from jax import lax
from jax.experimental import pallas as pl
from jax.experimental.pallas import tpu as pltpu
from jax.sharding import PartitionSpec as P

ITERS = 2
MESH = pl.DeviceIdType.MESH
VMEM = pl.BlockSpec(memory_space=pltpu.VMEM)
HBM = pl.BlockSpec(memory_space=pl.ANY)


def bit_of(me, bit):
    return lax.rem(lax.div(me, 1 << bit), 2)


def flip(me, bits):
    for bit in bits:
        me = me + (1 << bit) * (1 - 2 * bit_of(me, bit))
    return me


def enter(axes):
    barrier = pltpu.get_barrier_semaphore()
    count = 0
    for axis in axes:
        size = lax.axis_size(axis)
        me = lax.axis_index(axis)
        for other in range(1, size):
            pl.semaphore_signal(
                barrier, inc=1, device_id={axis: lax.rem(me + other, size)}, device_id_type=MESH
            )
        count += size - 1
    pl.semaphore_wait(barrier, count)


def remote(src, dst, send_sem, recv_sem, axis, target):
    return pltpu.make_async_remote_copy(
        src_ref=src,
        dst_ref=dst,
        send_sem=send_sem,
        recv_sem=recv_sem,
        device_id={axis: target},
        device_id_type=MESH,
    )


def held_bits(order, index):
    return [order[i] for i in range(len(order)) if index >> i & 1]


def gather_kernel(
    land, docs, proj, land_out, doc_out, proj_out,
    own_sem, land_send, land_recv, sib_send, sib_recv,
    doc_send, doc_recv, proj_send, proj_recv, psib_send, psib_recv,
):
    rows, cols = lax.axis_size("row"), lax.axis_size("col")
    me, z = lax.axis_index("row"), lax.axis_index("col")
    bits = rows.bit_length() - 1
    shards = rows // 2
    half = land.shape[1] // 2
    phalf = proj.shape[0] // 2
    upper = list(range(bits - 1, 0, -1))
    orders = [upper, upper[1:] + upper[:1]]
    sibling = flip(me, [0])
    enter(("row", "col"))

    locals_ = [
        pltpu.make_async_copy(land, land_out.at[me], own_sem.at[0]),
        pltpu.make_async_copy(docs, doc_out.at[z], own_sem.at[1]),
        pltpu.make_async_copy(proj, proj_out.at[z], own_sem.at[2]),
    ]
    sends = []

    def part(h):
        return pl.ds(h * half, half)

    def slot(h, j):
        return land_out.at[flip(me, held_bits(orders[h], j)), :, part(h)]

    def land_copy(h, j, stage):
        dst = j + (1 << stage)
        return remote(
            land.at[:, part(h)] if j == 0 else slot(h, j),
            slot(h, j),
            land_send.at[h, dst],
            land_recv.at[h, dst],
            "row",
            flip(me, [orders[h][stage]]),
        )

    def sib_copy(h, j):
        return remote(
            land.at[:, part(h)] if j == 0 else slot(h, j),
            slot(h, j), sib_send.at[h, j], sib_recv.at[h, j], "row", sibling,
        )

    def start(copy):
        copy.start()
        sends.append(copy)

    ph = pl.ds(pl.multiple_of(lax.rem(me, 2) * phalf, 8), phalf)
    ph_other = pl.ds(pl.multiple_of(lax.rem(me + 1, 2) * phalf, 8), phalf)

    def chain(d, t):
        sign = 1 - 2 * d
        origin = z - sign * t
        target = z + sign
        valid = (origin >= 0) & (origin < cols) & (target >= 0) & (target < cols)
        doc_src = docs if t == 0 else doc_out.at[origin]
        proj_src = proj.at[ph] if t == 0 else proj_out.at[origin, ph]
        return valid, (
            remote(doc_src, doc_out.at[origin], doc_send.at[d, t], doc_recv.at[d, t], "col", target),
            remote(proj_src, proj_out.at[origin, ph], proj_send.at[d, t], proj_recv.at[d, t], "col", target),
        )

    def arriving(d, t):
        sign = 1 - 2 * d
        origin = z - sign * (t + 1)
        valid = (origin >= 0) & (origin < cols)
        copies = (
            remote(doc_out.at[origin], doc_out.at[origin], doc_send.at[d, t], doc_recv.at[d, t], "col", z),
            remote(proj_out.at[origin, ph], proj_out.at[origin, ph], proj_send.at[d, t], proj_recv.at[d, t], "col", z),
        )
        share = remote(
            proj_out.at[origin, ph], proj_out.at[origin, ph],
            psib_send.at[d, t], psib_recv.at[d, t], "row", sibling,
        )
        incoming = remote(
            proj_out.at[origin, ph_other], proj_out.at[origin, ph_other],
            psib_send.at[d, t], psib_recv.at[d, t], "row", sibling,
        )
        return valid, copies, share, incoming

    for d in range(2):
        valid, copies = chain(d, 0)

        @pl.when(valid)
        def _():
            for copy in copies:
                copy.start()

    for stage in range(bits - 1):
        for h in range(2):
            start(land_copy(h, 0, stage))
    for h in range(2):
        start(sib_copy(h, 0))
    for copy in locals_:
        copy.start()

    def chain_step(t):
        for d in range(2):
            valid, copies, share, _ = arriving(d, t)

            @pl.when(valid)
            def _():
                for copy in copies:
                    copy.wait_recv()
                share.start()

            if t + 1 < cols - 1:
                onward, later = chain(d, t + 1)

                @pl.when(onward)
                def _():
                    for copy in later:
                        copy.start()

    def land_step(j):
        stage = j.bit_length() - 1
        for h in range(2):
            remote(slot(h, j), slot(h, j), land_send.at[h, j], land_recv.at[h, j], "row", me).wait_recv()
            for later in range(stage + 1, bits - 1):
                start(land_copy(h, j, later))
            start(sib_copy(h, j))

    for step in range(max(cols - 1, shards - 1)):
        if step < cols - 1:
            chain_step(step)
        if step + 1 < shards:
            land_step(step + 1)

    for h in range(2):
        for j in range(shards):
            dst = land_out.at[flip(me, [0] + held_bits(orders[h], j)), :, part(h)]
            remote(dst, dst, sib_send.at[h, j], sib_recv.at[h, j], "row", sibling).wait_recv()
    for copy in sends:
        copy.wait_send()
    for copy in locals_:
        copy.wait()
    for d in range(2):
        for t in range(cols - 1):
            valid, copies = chain(d, t)

            @pl.when(valid)
            def _():
                for copy in copies:
                    copy.wait_send()

            came, _, share, incoming = arriving(d, t)

            @pl.when(came)
            def _():
                incoming.wait_recv()
                share.wait_send()


def gather(rows, cols, land, docs, proj):
    shards = rows // 2
    dma = pltpu.SemaphoreType.DMA
    return pl.pallas_call(
        gather_kernel,
        out_shape=(
            jax.ShapeDtypeStruct((rows, *land.shape), land.dtype),
            jax.ShapeDtypeStruct((cols, *docs.shape), docs.dtype),
            jax.ShapeDtypeStruct((cols, *proj.shape), proj.dtype),
        ),
        in_specs=[VMEM] * 3,
        out_specs=(HBM,) * 3,
        scratch_shapes=[dma((3,))] + [dma((2, shards))] * 4 + [dma((2, cols - 1))] * 6,
        compiler_params=pltpu.CompilerParams(collective_id=0, has_side_effects=True),
        name="gather",
    )(land, docs, proj)


def halve(axis, orders, size, src, held, came, send_sem, recv_sem):
    me = lax.axis_index(axis)
    sections = range(len(orders))
    starts = [0 for _ in sections]
    for stage in range(len(orders[0])):
        length = size >> (stage + 1)
        copies, keeps = [], []
        for h in sections:
            mine = bit_of(me, orders[h][stage])
            base = h * size if stage == 0 else 0
            keep = pl.ds(pl.multiple_of(base + mine * length, 8), length)
            give = pl.ds(pl.multiple_of(base + (1 - mine) * length, 8), length)
            source = src.at[give] if stage == 0 else held[stage - 1].at[h, give]
            copy = remote(
                source, came[stage].at[h], send_sem.at[h, stage], recv_sem.at[h, stage],
                axis, flip(me, [orders[h][stage]]),
            )
            copy.start()
            copies.append(copy)
            keeps.append(keep)
            starts[h] = starts[h] + mine * length
        for h in sections:
            copies[h].wait_recv()
            old = src[keeps[h], :] if stage == 0 else held[stage - 1][h, keeps[h], :]
            held[stage][h] = old + came[stage][h]
        for copy in copies:
            copy.wait_send()
    return starts


def double(axis, orders, size, out, starts, send_sem, recv_sem):
    me = lax.axis_index(axis)
    sections = range(len(orders))
    starts = list(starts)
    for stage in reversed(range(len(orders[0]))):
        length = size >> (stage + 1)
        copies = []
        for h in sections:
            rows = pl.ds(pl.multiple_of(h * size + starts[h], 8), length)
            copy = remote(
                out.at[rows], out.at[rows], send_sem.at[h, stage], recv_sem.at[h, stage],
                axis, flip(me, [orders[h][stage]]),
            )
            copy.start()
            copies.append(copy)
        for h in sections:
            mine = bit_of(me, orders[h][stage])
            copies[h].wait_recv()
            starts[h] = starts[h] - mine * length
        for copy in copies:
            copy.wait_send()


def section_orders(count, sections):
    bits = count.bit_length() - 1
    upper = list(range(1, bits))
    return [[0] + upper[h % max(len(upper), 1):] + upper[: h % max(len(upper), 1)] for h in range(sections)]


def stage_scratch(sections, stages, size, width):
    shapes = [pltpu.VMEM((sections, size >> (stage + 1), width), jnp.float32) for stage in range(stages)]
    return shapes + shapes


def residual_kernel(orders, size, pred, labels, out, *scratch):
    stages = len(orders[0])
    held, came, sems = scratch[:stages], scratch[stages : 2 * stages], scratch[2 * stages :]
    enter(("col",))
    starts = halve("col", orders, size, pred, held, came, sems[0], sems[1])
    length = size >> stages
    for h in range(len(orders)):
        rows = pl.ds(pl.multiple_of(h * size + starts[h], 8), length)
        out[rows, :] = jax.nn.sigmoid(held[-1][h]) - labels[rows, :].astype(jnp.float32)
    double("col", orders, size, out, starts, sems[2], sems[3])


def residual_of(cols, pred, labels, collective_id):
    orders = [list(range(cols.bit_length() - 1))]
    stages = len(orders[0])
    dma = pltpu.SemaphoreType.DMA
    return pl.pallas_call(
        functools.partial(residual_kernel, orders, pred.shape[0]),
        out_shape=jax.ShapeDtypeStruct(pred.shape, jnp.float32),
        in_specs=[VMEM] * 2,
        out_specs=VMEM,
        scratch_shapes=stage_scratch(1, stages, *pred.shape) + [dma((1, stages))] * 4,
        compiler_params=pltpu.CompilerParams(collective_id=collective_id, has_side_effects=True),
        name=f"residual_{collective_id}",
    )(pred, labels)


def update_kernel(orders, size, step_size, product, current, out, *scratch):
    stages = len(orders[0])
    held, came, sems = scratch[:stages], scratch[stages : 2 * stages], scratch[2 * stages :]
    enter(("row",))
    starts = halve("row", orders, size, product, held, came, sems[0], sems[1])
    length = size >> stages
    for h in range(len(orders)):
        rows = pl.ds(pl.multiple_of(h * size + starts[h], 8), length)
        out[rows, :] = current[rows, :] - step_size * held[-1][h]
    double("row", orders, size, out, starts, sems[2], sems[3])


def update_of(rows, step_size, product, current, collective_id):
    sections = 2
    orders = section_orders(rows, sections)
    stages = len(orders[0])
    size = product.shape[0] // sections
    dma = pltpu.SemaphoreType.DMA
    return pl.pallas_call(
        functools.partial(update_kernel, orders, size, step_size),
        out_shape=jax.ShapeDtypeStruct(product.shape, jnp.float32),
        in_specs=[VMEM] * 2,
        out_specs=VMEM,
        scratch_shapes=stage_scratch(sections, stages, size, product.shape[1])
        + [dma((sections, stages))] * 4,
        compiler_params=pltpu.CompilerParams(collective_id=collective_id, has_side_effects=True),
        name=f"update_{collective_id}",
    )(product, current)


def gradient_kernel(orders, size, grad, out, *scratch):
    stages = len(orders[0])
    sections = len(orders)
    held, came = scratch[:stages], scratch[stages : 2 * stages]
    parts, send_sem, recv_sem, line_send, line_recv, deal_send, deal_recv, own_sem = scratch[2 * stages :]
    rows, cols = lax.axis_size("row"), lax.axis_size("col")
    me, z = lax.axis_index("row"), lax.axis_index("col")
    enter(("row", "col"))
    starts = halve("row", orders, size, grad, held, came, send_sem, recv_sem)
    length = size >> stages
    parts[z] = held[-1][...]

    def line(d, t):
        sign = 1 - 2 * d
        origin = z - sign * t
        target = z + sign
        valid = (origin >= 0) & (origin < cols) & (target >= 0) & (target < cols)
        return valid, remote(
            parts.at[origin], parts.at[origin], line_send.at[d, t], line_recv.at[d, t], "col", target
        )

    def deal(origin, index, action):
        for h in range(sections):
            target = origin * sections + h
            place = out.at[pl.ds(pl.multiple_of(starts[h], 8), length)]
            block = parts.at[origin, h]

            @pl.when(target != me)
            def _():
                copy = remote(block, place, deal_send.at[index, h], deal_recv.at[me], "row", target)
                if action == "start":
                    copy.start()
                else:
                    copy.wait_send()

            @pl.when(target == me)
            def _():
                copy = pltpu.make_async_copy(block, place, own_sem)
                if action == "start":
                    copy.start()
                else:
                    copy.wait()

    for d in range(2):
        valid, copy = line(d, 0)

        @pl.when(valid)
        def _():
            copy.start()

    deal(z, 0, "start")
    for t in range(cols - 1):
        for d in range(2):
            sign = 1 - 2 * d
            origin = z - sign * (t + 1)

            @pl.when((origin >= 0) & (origin < cols))
            def _():
                remote(
                    parts.at[origin], parts.at[origin], line_send.at[d, t], line_recv.at[d, t], "col", z
                ).wait_recv()

            if t + 1 < cols - 1:
                onward, later = line(d, t + 1)

                @pl.when(onward)
                def _():
                    later.start()

            @pl.when((origin >= 0) & (origin < cols))
            def _():
                deal(origin, 1 + 2 * t + d, "start")

    first = out.at[pl.ds(0, length)]
    for other in range(1, rows):
        source = lax.rem(me + other, rows)
        remote(first, first, deal_send.at[0, 0], deal_recv.at[source], "row", source).wait_recv()
    deal(z, 0, "wait")
    for t in range(cols - 1):
        for d in range(2):
            sign = 1 - 2 * d
            origin = z - sign * (t + 1)
            valid, copy = line(d, t)

            @pl.when(valid)
            def _():
                copy.wait_send()

            @pl.when((origin >= 0) & (origin < cols))
            def _():
                deal(origin, 1 + 2 * t + d, "wait")


def gradient_of(rows, cols, grad, collective_id):
    sections = rows // cols
    orders = section_orders(rows, sections)
    stages = len(orders[0])
    size = grad.shape[0] // sections
    width = grad.shape[1]
    dma = pltpu.SemaphoreType.DMA
    return pl.pallas_call(
        functools.partial(gradient_kernel, orders, size),
        out_shape=jax.ShapeDtypeStruct((size, width), jnp.float32),
        in_specs=[VMEM],
        out_specs=VMEM,
        scratch_shapes=stage_scratch(sections, stages, size, width)
        + [pltpu.VMEM((cols, sections, size >> stages, width), jnp.float32)]
        + [dma((sections, stages))] * 2
        + [dma((2, cols - 1))] * 2
        + [dma((2 * cols - 1, sections)), dma((rows,)), dma],
        compiler_params=pltpu.CompilerParams(collective_id=collective_id, has_side_effects=True),
        name=f"gradient_{collective_id}",
    )(grad)


def on_device(documents, projection, landmarks, coefficients, inverse_tiles, labels):
    high = lax.Precision.HIGH
    rows, cols = lax.axis_size("row"), lax.axis_size("col")
    land_t, docs_t, proj_full = gather(rows, cols, landmarks.T, documents.T, projection)
    land_t = land_t.reshape(-1, land_t.shape[2])
    docs_t = docs_t.reshape(-1, docs_t.shape[2])
    proj_full = proj_full.reshape(-1, proj_full.shape[2])
    feature_width = land_t.shape[0]

    def dot(a, b, over_a, over_b):
        return lax.dot_general(
            a, b, (((over_a,), (over_b,)), ((), ())), precision=high, preferred_element_type=jnp.float32
        )

    sq_land = jnp.sum(land_t * land_t, axis=0)
    rows_in = dot(docs_t, proj_full, 0, 0)
    sq_doc = jnp.sum(rows_in * rows_in, axis=1)
    inner = dot(rows_in, land_t, 1, 0)
    kernel = jnp.exp(-2.0 * (sq_doc[:, None] + sq_land[None, :] - 2.0 * inner) / feature_width)
    step_size = 64.0 / (documents.shape[0] * rows)
    current = coefficients
    residual = None
    for iteration in range(ITERS):
        first_id = 1 + 3 * iteration
        residual = residual_of(cols, dot(kernel, current, 1, 0), labels, first_id)
        gradient = gradient_of(rows, cols, dot(kernel, residual, 0, 0), first_id + 1)
        product = dot(inverse_tiles, gradient, 1, 0)
        current = update_of(rows, step_size, product, current, first_id + 2)
    return current, residual


def solution(mesh):
    in_specs = (
        P("row", "col"),
        P("col", None),
        P("col", "row"),
        P("col", None),
        P("col", "row"),
        P("row", None),
    )
    out_specs = (P("col", None), P("row", None))
    return jax.shard_map(
        on_device, mesh=mesh, in_specs=in_specs, out_specs=out_specs, check_vma=False
    )
```

```python
import functools

import jax
import jax.numpy as jnp
from jax import lax
from jax.experimental import pallas as pl
from jax.experimental.pallas import tpu as pltpu
from jax.sharding import PartitionSpec as P

ITERS = 2
MESH = pl.DeviceIdType.MESH
VMEM = pl.BlockSpec(memory_space=pltpu.VMEM)
HBM = pl.BlockSpec(memory_space=pl.ANY)


def bit_of(me, bit):
    return lax.rem(lax.div(me, 1 << bit), 2)


def flip(me, bits):
    for bit in bits:
        me = me + (1 << bit) * (1 - 2 * bit_of(me, bit))
    return me


def enter(axes):
    barrier = pltpu.get_barrier_semaphore()
    count = 0
    for axis in axes:
        size = lax.axis_size(axis)
        me = lax.axis_index(axis)
        for other in range(1, size):
            pl.semaphore_signal(
                barrier, inc=1, device_id={axis: lax.rem(me + other, size)}, device_id_type=MESH
            )
        count += size - 1
    pl.semaphore_wait(barrier, count)


def remote(src, dst, send_sem, recv_sem, axis, target):
    return pltpu.make_async_remote_copy(
        src_ref=src,
        dst_ref=dst,
        send_sem=send_sem,
        recv_sem=recv_sem,
        device_id={axis: target},
        device_id_type=MESH,
    )


def held_bits(order, index):
    return [order[i] for i in range(len(order)) if index >> i & 1]


def gather_kernel(
    land, docs, proj, land_out, doc_out, proj_out,
    own_sem, land_send, land_recv, sib_send, sib_recv,
    doc_send, doc_recv, proj_send, proj_recv, psib_send, psib_recv,
):
    rows, cols = lax.axis_size("row"), lax.axis_size("col")
    me, z = lax.axis_index("row"), lax.axis_index("col")
    bits = rows.bit_length() - 1
    shards = rows // 2
    half = land.shape[1] // 2
    phalf = proj.shape[0] // 2
    upper = list(range(bits - 1, 0, -1))
    orders = [upper, upper[1:] + upper[:1]]
    sibling = flip(me, [0])
    enter(("row", "col"))

    locals_ = [
        pltpu.make_async_copy(land, land_out.at[me], own_sem.at[0]),
        pltpu.make_async_copy(docs, doc_out.at[z], own_sem.at[1]),
        pltpu.make_async_copy(proj, proj_out.at[z], own_sem.at[2]),
    ]
    sends = []

    def part(h):
        return pl.ds(h * half, half)

    def slot(h, j):
        return land_out.at[flip(me, held_bits(orders[h], j)), :, part(h)]

    def land_copy(h, j, stage):
        dst = j + (1 << stage)
        return remote(
            land.at[:, part(h)] if j == 0 else slot(h, j),
            slot(h, j),
            land_send.at[h, dst],
            land_recv.at[h, dst],
            "row",
            flip(me, [orders[h][stage]]),
        )

    def sib_copy(h, j):
        return remote(
            land.at[:, part(h)] if j == 0 else slot(h, j),
            slot(h, j), sib_send.at[h, j], sib_recv.at[h, j], "row", sibling,
        )

    def start(copy):
        copy.start()
        sends.append(copy)

    ph = pl.ds(pl.multiple_of(lax.rem(me, 2) * phalf, 8), phalf)
    ph_other = pl.ds(pl.multiple_of(lax.rem(me + 1, 2) * phalf, 8), phalf)

    def chain(d, t):
        sign = 1 - 2 * d
        origin = z - sign * t
        target = z + sign
        valid = (origin >= 0) & (origin < cols) & (target >= 0) & (target < cols)
        doc_src = docs if t == 0 else doc_out.at[origin]
        proj_src = proj.at[ph] if t == 0 else proj_out.at[origin, ph]
        return valid, (
            remote(doc_src, doc_out.at[origin], doc_send.at[d, t], doc_recv.at[d, t], "col", target),
            remote(proj_src, proj_out.at[origin, ph], proj_send.at[d, t], proj_recv.at[d, t], "col", target),
        )

    def arriving(d, t):
        sign = 1 - 2 * d
        origin = z - sign * (t + 1)
        valid = (origin >= 0) & (origin < cols)
        copies = (
            remote(doc_out.at[origin], doc_out.at[origin], doc_send.at[d, t], doc_recv.at[d, t], "col", z),
            remote(proj_out.at[origin, ph], proj_out.at[origin, ph], proj_send.at[d, t], proj_recv.at[d, t], "col", z),
        )
        share = remote(
            proj_out.at[origin, ph], proj_out.at[origin, ph],
            psib_send.at[d, t], psib_recv.at[d, t], "row", sibling,
        )
        incoming = remote(
            proj_out.at[origin, ph_other], proj_out.at[origin, ph_other],
            psib_send.at[d, t], psib_recv.at[d, t], "row", sibling,
        )
        return valid, copies, share, incoming

    for d in range(2):
        valid, copies = chain(d, 0)

        @pl.when(valid)
        def _():
            for copy in copies:
                copy.start()

    for stage in range(bits - 1):
        for h in range(2):
            start(land_copy(h, 0, stage))
    for h in range(2):
        start(sib_copy(h, 0))
    for copy in locals_:
        copy.start()

    def chain_step(t):
        for d in range(2):
            valid, copies, share, _ = arriving(d, t)

            @pl.when(valid)
            def _():
                for copy in copies:
                    copy.wait_recv()
                share.start()

            if t + 1 < cols - 1:
                onward, later = chain(d, t + 1)

                @pl.when(onward)
                def _():
                    for copy in later:
                        copy.start()

    def land_step(j):
        stage = j.bit_length() - 1
        for h in range(2):
            remote(slot(h, j), slot(h, j), land_send.at[h, j], land_recv.at[h, j], "row", me).wait_recv()
            for later in range(stage + 1, bits - 1):
                start(land_copy(h, j, later))
            start(sib_copy(h, j))

    for step in range(max(cols - 1, shards - 1)):
        if step < cols - 1:
            chain_step(step)
        if step + 1 < shards:
            land_step(step + 1)

    for h in range(2):
        for j in range(shards):
            dst = land_out.at[flip(me, [0] + held_bits(orders[h], j)), :, part(h)]
            remote(dst, dst, sib_send.at[h, j], sib_recv.at[h, j], "row", sibling).wait_recv()
    for copy in sends:
        copy.wait_send()
    for copy in locals_:
        copy.wait()
    for d in range(2):
        for t in range(cols - 1):
            valid, copies = chain(d, t)

            @pl.when(valid)
            def _():
                for copy in copies:
                    copy.wait_send()

            came, _, share, incoming = arriving(d, t)

            @pl.when(came)
            def _():
                incoming.wait_recv()
                share.wait_send()


def gather(rows, cols, land, docs, proj):
    shards = rows // 2
    dma = pltpu.SemaphoreType.DMA
    return pl.pallas_call(
        gather_kernel,
        out_shape=(
            jax.ShapeDtypeStruct((rows, *land.shape), land.dtype),
            jax.ShapeDtypeStruct((cols, *docs.shape), docs.dtype),
            jax.ShapeDtypeStruct((cols, *proj.shape), proj.dtype),
        ),
        in_specs=[VMEM] * 3,
        out_specs=(HBM,) * 3,
        scratch_shapes=[dma((3,))] + [dma((2, shards))] * 4 + [dma((2, cols - 1))] * 6,
        compiler_params=pltpu.CompilerParams(collective_id=0, has_side_effects=True),
        name="gather",
    )(land, docs, proj)


def section_orders(count, sections):
    bits = count.bit_length() - 1
    upper = list(range(1, bits))
    return [[0] + upper[h % max(len(upper), 1):] + upper[: h % max(len(upper), 1)] for h in range(sections)]


def group_count(length, blocks, most):
    return max(1, min(most, length // (blocks * 8)))


def waves(groups, stages, finish, begin):
    for wave in range(stages + groups):
        for group in range(groups):
            stage = wave - group
            if 0 <= stage - 1 < stages:
                finish(group, stage - 1)
            if 0 <= stage < stages:
                begin(group, stage)


class Halving:
    def __init__(self, axis, orders, size, bases, src, held, came, send_sem, recv_sem):
        self.axis, self.orders, self.size, self.bases, self.src = axis, orders, size, bases, src
        self.held, self.came, self.send_sem, self.recv_sem = held, came, send_sem, recv_sem
        self.me = lax.axis_index(axis)
        self.starts = [0 for _ in bases]
        self.pending, self.sent = {}, []

    def begin(self, n, stage):
        order = self.orders[n]
        length = self.size >> (stage + 1)
        mine = bit_of(self.me, order[stage])
        base = self.bases[n] if stage == 0 else 0
        keep = pl.ds(pl.multiple_of(base + mine * length, 8), length)
        give = pl.ds(pl.multiple_of(base + (1 - mine) * length, 8), length)
        copy = remote(
            self.src.at[give] if stage == 0 else self.held[stage - 1].at[n, give],
            self.came[stage].at[n], self.send_sem.at[n, stage], self.recv_sem.at[n, stage],
            self.axis, flip(self.me, [order[stage]]),
        )
        copy.start()
        self.starts[n] = self.starts[n] + mine * length
        self.pending[n] = (copy, keep)
        self.sent.append(copy)

    def finish(self, n, stage):
        copy, keep = self.pending[n]
        copy.wait_recv()
        old = self.src[keep, :] if stage == 0 else self.held[stage - 1][n, keep, :]
        self.held[stage][n] = old + self.came[stage][n]

    def end(self):
        for copy in self.sent:
            copy.wait_send()


def stage_scratch(sections, stages, size, width):
    shapes = [pltpu.VMEM((sections, size >> (stage + 1), width), jnp.float32) for stage in range(stages)]
    return shapes + shapes


def reduced_kernel(axis, orders, size, groups, apply, src, other, out, *scratch):
    stages = len(orders[0])
    per_group = len(orders) // groups
    held, came, sems = scratch[:stages], scratch[stages : 2 * stages], scratch[2 * stages :]
    me = lax.axis_index(axis)
    bases = [n * size for n in range(len(orders))]
    enter((axis,))
    sums = Halving(axis, orders, size, bases, src, held, came, sems[0], sems[1])
    block = size >> stages
    pending, sent = {}, []

    def members(group):
        return range(group * per_group, (group + 1) * per_group)

    def finish(group, stage):
        for n in members(group):
            if stage < stages:
                sums.finish(n, stage)
                if stage == stages - 1:
                    rows = pl.ds(pl.multiple_of(bases[n] + sums.starts[n], 8), block)
                    out[rows, :] = apply(held[-1][n], other[rows, :])
            else:
                back = 2 * stages - 1 - stage
                pending[n].wait_recv()
                sums.starts[n] = sums.starts[n] - bit_of(me, orders[n][back]) * (size >> (back + 1))

    def begin(group, stage):
        for n in members(group):
            if stage < stages:
                sums.begin(n, stage)
            else:
                back = 2 * stages - 1 - stage
                rows = pl.ds(pl.multiple_of(bases[n] + sums.starts[n], 8), size >> (back + 1))
                copy = remote(
                    out.at[rows], out.at[rows], sems[2].at[n, back], sems[3].at[n, back],
                    axis, flip(me, [orders[n][back]]),
                )
                copy.start()
                pending[n] = copy
                sent.append(copy)

    waves(groups, 2 * stages, finish, begin)
    sums.end()
    for copy in sent:
        copy.wait_send()


def reduced(axis, orders, groups, apply, src, other, collective_id, name):
    sections = len(orders)
    stages = len(orders[0])
    size = src.shape[0] // sections
    dma = pltpu.SemaphoreType.DMA
    return pl.pallas_call(
        functools.partial(reduced_kernel, axis, orders, size, groups, apply),
        out_shape=jax.ShapeDtypeStruct(src.shape, jnp.float32),
        in_specs=[VMEM] * 2,
        out_specs=VMEM,
        scratch_shapes=stage_scratch(sections, stages, size, src.shape[1]) + [dma((sections, stages))] * 4,
        compiler_params=pltpu.CompilerParams(collective_id=collective_id, has_side_effects=True),
        name=f"{name}_{collective_id}",
    )(src, other)


def residual_of(cols, pred, labels, collective_id):
    groups = group_count(pred.shape[0], cols, 2)
    orders = [list(range(cols.bit_length() - 1))] * groups

    def apply(total, target):
        return jax.nn.sigmoid(total) - target.astype(jnp.float32)

    return reduced("col", orders, groups, apply, pred, labels, collective_id, "residual")


def update_of(rows, step_size, product, current, collective_id):
    groups = group_count(product.shape[0], 2 * rows, 4)

    def apply(total, old):
        return old - step_size * total

    return reduced(
        "row", section_orders(rows, 2) * groups, groups, apply, product, current, collective_id, "update"
    )


def gradient_kernel(orders, size, groups, grad, out, *scratch):
    stages = len(orders[0])
    halves = len(orders)
    held, came = scratch[:stages], scratch[stages : 2 * stages]
    parts, send_sem, recv_sem, line_send, line_recv, deal_send, deal_recv, own_sem = scratch[2 * stages :]
    rows, cols = lax.axis_size("row"), lax.axis_size("col")
    me, z = lax.axis_index("row"), lax.axis_index("col")
    enter(("row", "col"))
    bases = [(h * groups + g) * size for g in range(groups) for h in range(halves)]
    sums = Halving("row", orders * groups, size, bases, grad, held, came, send_sem, recv_sem)
    length = size >> stages

    def line(g, d, t):
        sign = 1 - 2 * d
        origin = z - sign * t
        target = z + sign
        valid = (origin >= 0) & (origin < cols) & (target >= 0) & (target < cols)
        return valid, remote(
            parts.at[g, origin], parts.at[g, origin], line_send.at[g, d, t], line_recv.at[g, d, t], "col", target
        )

    def came_from(d, t):
        origin = z - (1 - 2 * d) * (t + 1)
        return (origin >= 0) & (origin < cols), origin

    def deal(g, origin, index, first):
        for h in range(halves):
            target = origin * halves + h
            place = out.at[pl.ds(pl.multiple_of(g * size + sums.starts[g * halves + h], 8), length)]
            block = parts.at[g, origin, h]

            @pl.when(target != me)
            def _():
                copy = remote(block, place, deal_send.at[g, index, h], deal_recv.at[g, me], "row", target)
                if first:
                    copy.start()
                else:
                    copy.wait_send()

            @pl.when(target == me)
            def _():
                copy = pltpu.make_async_copy(block, place, own_sem.at[g])
                if first:
                    copy.start()
                else:
                    copy.wait()

    def finish(g, stage):
        if stage < stages:
            for h in range(halves):
                sums.finish(g * halves + h, stage)
                if stage == stages - 1:
                    parts[g, z, h] = held[-1][g * halves + h]
            return
        t = stage - stages
        for d in range(2):
            valid, origin = came_from(d, t)

            @pl.when(valid)
            def _():
                remote(
                    parts.at[g, origin], parts.at[g, origin], line_send.at[g, d, t], line_recv.at[g, d, t], "col", z
                ).wait_recv()

            if t + 1 < cols - 1:
                onward, later = line(g, d, t + 1)

                @pl.when(onward)
                def _():
                    later.start()

            @pl.when(valid)
            def _():
                deal(g, origin, 1 + 2 * t + d, True)

    def begin(g, stage):
        if stage < stages:
            for h in range(halves):
                sums.begin(g * halves + h, stage)
        elif stage == stages:
            for d in range(2):
                valid, copy = line(g, d, 0)

                @pl.when(valid)
                def _():
                    copy.start()

            deal(g, z, 0, True)

    waves(groups, stages + cols - 1, finish, begin)
    for g in range(groups):
        first = out.at[pl.ds(0, length)]
        for other in range(1, rows):
            source = lax.rem(me + other, rows)
            remote(first, first, deal_send.at[g, 0, 0], deal_recv.at[g, source], "row", source).wait_recv()
    sums.end()
    for g in range(groups):
        deal(g, z, 0, False)
        for t in range(cols - 1):
            for d in range(2):
                valid, copy = line(g, d, t)

                @pl.when(valid)
                def _():
                    copy.wait_send()

                arrived, origin = came_from(d, t)

                @pl.when(arrived)
                def _():
                    deal(g, origin, 1 + 2 * t + d, False)


def gradient_of(rows, cols, grad, collective_id):
    halves = rows // cols
    orders = section_orders(rows, halves)
    stages = len(orders[0])
    width = grad.shape[1]
    groups = group_count(grad.shape[0], halves * rows, 4)
    size = grad.shape[0] // (halves * groups)
    sections = halves * groups
    dma = pltpu.SemaphoreType.DMA
    return pl.pallas_call(
        functools.partial(gradient_kernel, orders, size, groups),
        out_shape=jax.ShapeDtypeStruct((size * groups, width), jnp.float32),
        in_specs=[VMEM],
        out_specs=VMEM,
        scratch_shapes=stage_scratch(sections, stages, size, width)
        + [pltpu.VMEM((groups, cols, halves, size >> stages, width), jnp.float32)]
        + [dma((sections, stages))] * 2
        + [dma((groups, 2, cols - 1))] * 2
        + [dma((groups, 2 * cols - 1, halves)), dma((groups, rows)), dma((groups,))],
        compiler_params=pltpu.CompilerParams(collective_id=collective_id, has_side_effects=True),
        name=f"gradient_{collective_id}",
    )(grad)


def split(x):
    high = x.astype(jnp.bfloat16)
    return high, (x - high.astype(jnp.float32)).astype(jnp.bfloat16)


def product_kernel(tile, grad, out, both):
    width = grad.shape[1]

    @pl.when(pl.program_id(0) == 0)
    def _():
        high, low = split(grad[...])
        both[:, :width] = high
        both[:, width:] = low

    high, low = split(tile[...])
    wide = jnp.dot(high, both[...], preferred_element_type=jnp.float32)
    out[...] = (
        wide[:, :width]
        + wide[:, width:]
        + jnp.dot(low, both[:, :width], preferred_element_type=jnp.float32)
    )


def product_of(tiles, grad):
    length, depth = tiles.shape
    width = grad.shape[1]
    step = min(512, length)
    return pl.pallas_call(
        product_kernel,
        grid=(length // step,),
        out_shape=jax.ShapeDtypeStruct((length, width), jnp.float32),
        in_specs=[
            pl.BlockSpec((step, depth), lambda i: (i, 0)),
            pl.BlockSpec((depth, width), lambda i: (0, 0)),
        ],
        out_specs=pl.BlockSpec((step, width), lambda i: (i, 0)),
        scratch_shapes=[pltpu.VMEM((depth, 2 * width), jnp.bfloat16)],
        cost_estimate=pl.CostEstimate(
            flops=6 * length * depth * width, bytes_accessed=4 * length * depth, transcendentals=0
        ),
        name="product",
    )(tiles, grad)


def on_device(documents, projection, landmarks, coefficients, inverse_tiles, labels):
    high = lax.Precision.HIGH
    rows, cols = lax.axis_size("row"), lax.axis_size("col")
    land_t, docs_t, proj_full = gather(rows, cols, landmarks.T, documents.T, projection)
    land_t = land_t.reshape(-1, land_t.shape[2])
    docs_t = docs_t.reshape(-1, docs_t.shape[2])
    proj_full = proj_full.reshape(-1, proj_full.shape[2])
    feature_width = land_t.shape[0]

    def dot(a, b, over_a, over_b):
        return lax.dot_general(
            a, b, (((over_a,), (over_b,)), ((), ())), precision=high, preferred_element_type=jnp.float32
        )

    sq_land = jnp.sum(land_t * land_t, axis=0)
    rows_in = dot(docs_t, proj_full, 0, 0)
    sq_doc = jnp.sum(rows_in * rows_in, axis=1)
    inner = dot(rows_in, land_t, 1, 0)
    kernel = jnp.exp(-2.0 * (sq_doc[:, None] + sq_land[None, :] - 2.0 * inner) / feature_width)
    step_size = 64.0 / (documents.shape[0] * rows)
    current = coefficients
    residual = None
    for iteration in range(ITERS):
        first_id = 1 + 3 * iteration
        residual = residual_of(cols, dot(kernel, current, 1, 0), labels, first_id)
        gradient = gradient_of(rows, cols, dot(kernel, residual, 0, 0), first_id + 1)
        product = product_of(inverse_tiles, gradient)
        current = update_of(rows, step_size, product, current, first_id + 2)
    return current, residual


def solution(mesh):
    in_specs = (
        P("row", "col"),
        P("col", None),
        P("col", "row"),
        P("col", None),
        P("col", "row"),
        P("row", None),
    )
    out_specs = (P("col", None), P("row", None))
    return jax.shard_map(
        on_device, mesh=mesh, in_specs=in_specs, out_specs=out_specs, check_vma=False
    )
```

```python
import functools

import jax
import jax.numpy as jnp
from jax import lax
from jax.experimental import pallas as pl
from jax.experimental.pallas import tpu as pltpu
from jax.sharding import PartitionSpec as P

ITERS = 2
MESH = pl.DeviceIdType.MESH
VMEM = pl.BlockSpec(memory_space=pltpu.VMEM)
HBM = pl.BlockSpec(memory_space=pl.ANY)


def bit_of(me, bit):
    return lax.rem(lax.div(me, 1 << bit), 2)


def flip(me, bits):
    for bit in bits:
        me = me + (1 << bit) * (1 - 2 * bit_of(me, bit))
    return me


def enter(axes):
    barrier = pltpu.get_barrier_semaphore()
    count = 0
    for axis in axes:
        size = lax.axis_size(axis)
        me = lax.axis_index(axis)
        for other in range(1, size):
            pl.semaphore_signal(
                barrier, inc=1, device_id={axis: lax.rem(me + other, size)}, device_id_type=MESH
            )
        count += size - 1
    pl.semaphore_wait(barrier, count)


def remote(src, dst, send_sem, recv_sem, axis, target):
    return pltpu.make_async_remote_copy(
        src_ref=src,
        dst_ref=dst,
        send_sem=send_sem,
        recv_sem=recv_sem,
        device_id={axis: target},
        device_id_type=MESH,
    )


def held_bits(order, index):
    return [order[i] for i in range(len(order)) if index >> i & 1]


def gather_kernel(
    land, docs, proj, land_out, doc_out, proj_out,
    own_sem, land_send, land_recv, sib_send, sib_recv,
    doc_send, doc_recv, proj_send, proj_recv, psib_send, psib_recv,
):
    rows, cols = lax.axis_size("row"), lax.axis_size("col")
    me, z = lax.axis_index("row"), lax.axis_index("col")
    bits = rows.bit_length() - 1
    shards = rows // 2
    half = land.shape[1] // 2
    phalf = proj.shape[0] // 2
    upper = list(range(bits - 1, 0, -1))
    orders = [upper, upper[1:] + upper[:1]]
    sibling = flip(me, [0])
    enter(("row", "col"))

    locals_ = [
        pltpu.make_async_copy(land, land_out.at[me], own_sem.at[0]),
        pltpu.make_async_copy(docs, doc_out.at[z], own_sem.at[1]),
        pltpu.make_async_copy(proj, proj_out.at[z], own_sem.at[2]),
    ]
    sends = []

    def part(h):
        return pl.ds(h * half, half)

    def slot(h, j):
        return land_out.at[flip(me, held_bits(orders[h], j)), :, part(h)]

    def land_copy(h, j, stage):
        dst = j + (1 << stage)
        return remote(
            land.at[:, part(h)] if j == 0 else slot(h, j),
            slot(h, j),
            land_send.at[h, dst],
            land_recv.at[h, dst],
            "row",
            flip(me, [orders[h][stage]]),
        )

    def sib_copy(h, j):
        return remote(
            land.at[:, part(h)] if j == 0 else slot(h, j),
            slot(h, j), sib_send.at[h, j], sib_recv.at[h, j], "row", sibling,
        )

    def start(copy):
        copy.start()
        sends.append(copy)

    ph = pl.ds(pl.multiple_of(lax.rem(me, 2) * phalf, 8), phalf)
    ph_other = pl.ds(pl.multiple_of(lax.rem(me + 1, 2) * phalf, 8), phalf)

    def chain(d, t):
        sign = 1 - 2 * d
        origin = z - sign * t
        target = z + sign
        valid = (origin >= 0) & (origin < cols) & (target >= 0) & (target < cols)
        doc_src = docs if t == 0 else doc_out.at[origin]
        proj_src = proj.at[ph] if t == 0 else proj_out.at[origin, ph]
        return valid, (
            remote(doc_src, doc_out.at[origin], doc_send.at[d, t], doc_recv.at[d, t], "col", target),
            remote(proj_src, proj_out.at[origin, ph], proj_send.at[d, t], proj_recv.at[d, t], "col", target),
        )

    def arriving(d, t):
        sign = 1 - 2 * d
        origin = z - sign * (t + 1)
        valid = (origin >= 0) & (origin < cols)
        copies = (
            remote(doc_out.at[origin], doc_out.at[origin], doc_send.at[d, t], doc_recv.at[d, t], "col", z),
            remote(proj_out.at[origin, ph], proj_out.at[origin, ph], proj_send.at[d, t], proj_recv.at[d, t], "col", z),
        )
        share = remote(
            proj_out.at[origin, ph], proj_out.at[origin, ph],
            psib_send.at[d, t], psib_recv.at[d, t], "row", sibling,
        )
        incoming = remote(
            proj_out.at[origin, ph_other], proj_out.at[origin, ph_other],
            psib_send.at[d, t], psib_recv.at[d, t], "row", sibling,
        )
        return valid, copies, share, incoming

    for d in range(2):
        valid, copies = chain(d, 0)

        @pl.when(valid)
        def _():
            for copy in copies:
                copy.start()

    for stage in range(bits - 1):
        for h in range(2):
            start(land_copy(h, 0, stage))
    for h in range(2):
        start(sib_copy(h, 0))
    for copy in locals_:
        copy.start()

    def chain_step(t):
        for d in range(2):
            valid, copies, share, _ = arriving(d, t)

            @pl.when(valid)
            def _():
                for copy in copies:
                    copy.wait_recv()
                share.start()

            if t + 1 < cols - 1:
                onward, later = chain(d, t + 1)

                @pl.when(onward)
                def _():
                    for copy in later:
                        copy.start()

    def land_step(j):
        stage = j.bit_length() - 1
        for h in range(2):
            remote(slot(h, j), slot(h, j), land_send.at[h, j], land_recv.at[h, j], "row", me).wait_recv()
            for later in range(stage + 1, bits - 1):
                start(land_copy(h, j, later))
            start(sib_copy(h, j))

    for step in range(max(cols - 1, shards - 1)):
        if step < cols - 1:
            chain_step(step)
        if step + 1 < shards:
            land_step(step + 1)

    for h in range(2):
        for j in range(shards):
            dst = land_out.at[flip(me, [0] + held_bits(orders[h], j)), :, part(h)]
            remote(dst, dst, sib_send.at[h, j], sib_recv.at[h, j], "row", sibling).wait_recv()
    for copy in sends:
        copy.wait_send()
    for copy in locals_:
        copy.wait()
    for d in range(2):
        for t in range(cols - 1):
            valid, copies = chain(d, t)

            @pl.when(valid)
            def _():
                for copy in copies:
                    copy.wait_send()

            came, _, share, incoming = arriving(d, t)

            @pl.when(came)
            def _():
                incoming.wait_recv()
                share.wait_send()


def gather(rows, cols, land, docs, proj):
    shards = rows // 2
    dma = pltpu.SemaphoreType.DMA
    return pl.pallas_call(
        gather_kernel,
        out_shape=(
            jax.ShapeDtypeStruct((rows, *land.shape), land.dtype),
            jax.ShapeDtypeStruct((cols, *docs.shape), docs.dtype),
            jax.ShapeDtypeStruct((cols, *proj.shape), proj.dtype),
        ),
        in_specs=[VMEM] * 3,
        out_specs=(HBM,) * 3,
        scratch_shapes=[dma((3,))] + [dma((2, shards))] * 4 + [dma((2, cols - 1))] * 6,
        compiler_params=pltpu.CompilerParams(collective_id=0, has_side_effects=True),
        name="gather",
    )(land, docs, proj)


def section_orders(count, sections):
    bits = count.bit_length() - 1
    upper = list(range(1, bits))
    return [[0] + upper[h % max(len(upper), 1):] + upper[: h % max(len(upper), 1)] for h in range(sections)]


def group_count(length, blocks, most):
    return max(1, min(most, length // (blocks * 8)))


def waves(groups, stages, finish, begin):
    for wave in range(stages + groups):
        for group in range(groups):
            stage = wave - group
            if 0 <= stage - 1 < stages:
                finish(group, stage - 1)
            if 0 <= stage < stages:
                begin(group, stage)


class Halving:
    def __init__(self, axis, orders, size, bases, src, held, came, send_sem, recv_sem):
        self.axis, self.orders, self.size, self.bases, self.src = axis, orders, size, bases, src
        self.held, self.came, self.send_sem, self.recv_sem = held, came, send_sem, recv_sem
        self.me = lax.axis_index(axis)
        self.starts = [0 for _ in bases]
        self.pending, self.sent = {}, []

    def begin(self, n, stage):
        order = self.orders[n]
        length = self.size >> (stage + 1)
        mine = bit_of(self.me, order[stage])
        base = self.bases[n] if stage == 0 else 0
        keep = pl.ds(pl.multiple_of(base + mine * length, 8), length)
        give = pl.ds(pl.multiple_of(base + (1 - mine) * length, 8), length)
        copy = remote(
            self.src.at[give] if stage == 0 else self.held[stage - 1].at[n, give],
            self.came[stage].at[n], self.send_sem.at[n, stage], self.recv_sem.at[n, stage],
            self.axis, flip(self.me, [order[stage]]),
        )
        copy.start()
        self.starts[n] = self.starts[n] + mine * length
        self.pending[n] = (copy, keep)
        self.sent.append(copy)

    def finish(self, n, stage):
        copy, keep = self.pending[n]
        copy.wait_recv()
        old = self.src[keep, :] if stage == 0 else self.held[stage - 1][n, keep, :]
        self.held[stage][n] = old + self.came[stage][n]

    def end(self):
        for copy in self.sent:
            copy.wait_send()


def stage_scratch(sections, stages, size, width):
    shapes = [pltpu.VMEM((sections, size >> (stage + 1), width), jnp.float32) for stage in range(stages)]
    return shapes + shapes


def reduced_kernel(axis, orders, size, groups, apply, src, other, out, *scratch):
    stages = len(orders[0])
    per_group = len(orders) // groups
    held, came, sems = scratch[:stages], scratch[stages : 2 * stages], scratch[2 * stages :]
    me = lax.axis_index(axis)
    bases = [n * size for n in range(len(orders))]
    enter((axis,))
    sums = Halving(axis, orders, size, bases, src, held, came, sems[0], sems[1])
    block = size >> stages
    pending, sent = {}, []

    def members(group):
        return range(group * per_group, (group + 1) * per_group)

    def finish(group, stage):
        for n in members(group):
            if stage < stages:
                sums.finish(n, stage)
                if stage == stages - 1:
                    rows = pl.ds(pl.multiple_of(bases[n] + sums.starts[n], 8), block)
                    out[rows, :] = apply(held[-1][n], other[rows, :])
            else:
                back = 2 * stages - 1 - stage
                pending[n].wait_recv()
                sums.starts[n] = sums.starts[n] - bit_of(me, orders[n][back]) * (size >> (back + 1))

    def begin(group, stage):
        for n in members(group):
            if stage < stages:
                sums.begin(n, stage)
            else:
                back = 2 * stages - 1 - stage
                rows = pl.ds(pl.multiple_of(bases[n] + sums.starts[n], 8), size >> (back + 1))
                copy = remote(
                    out.at[rows], out.at[rows], sems[2].at[n, back], sems[3].at[n, back],
                    axis, flip(me, [orders[n][back]]),
                )
                copy.start()
                pending[n] = copy
                sent.append(copy)

    waves(groups, 2 * stages, finish, begin)
    sums.end()
    for copy in sent:
        copy.wait_send()


def reduced(axis, orders, groups, apply, src, other, collective_id, name):
    sections = len(orders)
    stages = len(orders[0])
    size = src.shape[0] // sections
    dma = pltpu.SemaphoreType.DMA
    return pl.pallas_call(
        functools.partial(reduced_kernel, axis, orders, size, groups, apply),
        out_shape=jax.ShapeDtypeStruct(src.shape, jnp.float32),
        in_specs=[VMEM] * 2,
        out_specs=VMEM,
        scratch_shapes=stage_scratch(sections, stages, size, src.shape[1]) + [dma((sections, stages))] * 4,
        compiler_params=pltpu.CompilerParams(collective_id=collective_id, has_side_effects=True),
        name=f"{name}_{collective_id}",
    )(src, other)


def residual_of(cols, pred, labels, collective_id):
    groups = group_count(pred.shape[0], cols, 2)
    orders = [list(range(cols.bit_length() - 1))] * groups

    def apply(total, target):
        return jax.nn.sigmoid(total) - target.astype(jnp.float32)

    return reduced("col", orders, groups, apply, pred, labels, collective_id, "residual")


def update_of(rows, step_size, product, current, collective_id):
    groups = group_count(product.shape[0], 2 * rows, 4)

    def apply(total, old):
        return old - step_size * total

    return reduced(
        "row", section_orders(rows, 2) * groups, groups, apply, product, current, collective_id, "update"
    )


def gradient_kernel(orders, size, groups, grad, out, *scratch):
    stages = len(orders[0])
    halves = len(orders)
    held, came = scratch[:stages], scratch[stages : 2 * stages]
    parts, send_sem, recv_sem, line_send, line_recv, deal_send, deal_recv, own_sem = scratch[2 * stages :]
    rows, cols = lax.axis_size("row"), lax.axis_size("col")
    me, z = lax.axis_index("row"), lax.axis_index("col")
    enter(("row", "col"))
    bases = [(h * groups + g) * size for g in range(groups) for h in range(halves)]
    sums = Halving("row", orders * groups, size, bases, grad, held, came, send_sem, recv_sem)
    length = size >> stages

    def line(g, d, t):
        sign = 1 - 2 * d
        origin = z - sign * t
        target = z + sign
        valid = (origin >= 0) & (origin < cols) & (target >= 0) & (target < cols)
        return valid, remote(
            parts.at[g, origin], parts.at[g, origin], line_send.at[g, d, t], line_recv.at[g, d, t], "col", target
        )

    def came_from(d, t):
        origin = z - (1 - 2 * d) * (t + 1)
        return (origin >= 0) & (origin < cols), origin

    def deal(g, origin, index, first):
        for h in range(halves):
            target = origin * halves + h
            place = out.at[pl.ds(pl.multiple_of(g * size + sums.starts[g * halves + h], 8), length)]
            block = parts.at[g, origin, h]

            @pl.when(target != me)
            def _():
                copy = remote(block, place, deal_send.at[g, index, h], deal_recv.at[g, me], "row", target)
                if first:
                    copy.start()
                else:
                    copy.wait_send()

            @pl.when(target == me)
            def _():
                copy = pltpu.make_async_copy(block, place, own_sem.at[g])
                if first:
                    copy.start()
                else:
                    copy.wait()

    def finish(g, stage):
        if stage < stages:
            for h in range(halves):
                sums.finish(g * halves + h, stage)
                if stage == stages - 1:
                    parts[g, z, h] = held[-1][g * halves + h]
            return
        t = stage - stages
        for d in range(2):
            valid, origin = came_from(d, t)

            @pl.when(valid)
            def _():
                remote(
                    parts.at[g, origin], parts.at[g, origin], line_send.at[g, d, t], line_recv.at[g, d, t], "col", z
                ).wait_recv()

            if t + 1 < cols - 1:
                onward, later = line(g, d, t + 1)

                @pl.when(onward)
                def _():
                    later.start()

            @pl.when(valid)
            def _():
                deal(g, origin, 1 + 2 * t + d, True)

    def begin(g, stage):
        if stage < stages:
            for h in range(halves):
                sums.begin(g * halves + h, stage)
        elif stage == stages:
            for d in range(2):
                valid, copy = line(g, d, 0)

                @pl.when(valid)
                def _():
                    copy.start()

            deal(g, z, 0, True)

    waves(groups, stages + cols - 1, finish, begin)
    for g in range(groups):
        first = out.at[pl.ds(0, length)]
        for other in range(1, rows):
            source = lax.rem(me + other, rows)
            remote(first, first, deal_send.at[g, 0, 0], deal_recv.at[g, source], "row", source).wait_recv()
    sums.end()
    for g in range(groups):
        deal(g, z, 0, False)
        for t in range(cols - 1):
            for d in range(2):
                valid, copy = line(g, d, t)

                @pl.when(valid)
                def _():
                    copy.wait_send()

                arrived, origin = came_from(d, t)

                @pl.when(arrived)
                def _():
                    deal(g, origin, 1 + 2 * t + d, False)


def gradient_of(rows, cols, grad, collective_id):
    halves = rows // cols
    orders = section_orders(rows, halves)
    stages = len(orders[0])
    width = grad.shape[1]
    groups = group_count(grad.shape[0], halves * rows, 4)
    size = grad.shape[0] // (halves * groups)
    sections = halves * groups
    dma = pltpu.SemaphoreType.DMA
    return pl.pallas_call(
        functools.partial(gradient_kernel, orders, size, groups),
        out_shape=jax.ShapeDtypeStruct((size * groups, width), jnp.float32),
        in_specs=[VMEM],
        out_specs=VMEM,
        scratch_shapes=stage_scratch(sections, stages, size, width)
        + [pltpu.VMEM((groups, cols, halves, size >> stages, width), jnp.float32)]
        + [dma((sections, stages))] * 2
        + [dma((groups, 2, cols - 1))] * 2
        + [dma((groups, 2 * cols - 1, halves)), dma((groups, rows)), dma((groups,))],
        compiler_params=pltpu.CompilerParams(collective_id=collective_id, has_side_effects=True),
        name=f"gradient_{collective_id}",
    )(grad)


def split(x):
    high = x.astype(jnp.bfloat16)
    return high, (x - high.astype(jnp.float32)).astype(jnp.bfloat16)


def product_kernel(tile, grad, out, both):
    width = grad.shape[1]

    @pl.when(pl.program_id(0) == 0)
    def _():
        high, low = split(grad[...])
        both[:, :width] = high
        both[:, width:] = low

    high, low = split(tile[...])
    wide = jnp.dot(high, both[...], preferred_element_type=jnp.float32)
    out[...] = (
        wide[:, :width]
        + wide[:, width:]
        + jnp.dot(low, both[:, :width], preferred_element_type=jnp.float32)
    )


def product_of(tiles, grad):
    length, depth = tiles.shape
    width = grad.shape[1]
    step = min(512, length)
    return pl.pallas_call(
        product_kernel,
        grid=(length // step,),
        out_shape=jax.ShapeDtypeStruct((length, width), jnp.float32),
        in_specs=[
            pl.BlockSpec((step, depth), lambda i: (i, 0)),
            pl.BlockSpec((depth, width), lambda i: (0, 0)),
        ],
        out_specs=pl.BlockSpec((step, width), lambda i: (i, 0)),
        scratch_shapes=[pltpu.VMEM((depth, 2 * width), jnp.bfloat16)],
        cost_estimate=pl.CostEstimate(
            flops=6 * length * depth * width, bytes_accessed=4 * length * depth, transcendentals=0
        ),
        name="product",
    )(tiles, grad)


def kernel_kernel(proj, land, current, out, pred, high_ref, low_ref, square_ref):
    features = land.shape[0]

    @pl.when(pl.program_id(0) == 0)
    def _():
        rows = proj[...]
        high_ref[...], low_ref[...] = split(rows)
        square_ref[...] = jnp.sum(rows * rows, axis=1, keepdims=True)
        pred[...] = jnp.zeros_like(pred)

    def dots(a_high, a_low, b_high, b_low):
        def one(a, b):
            return jnp.dot(a, b, preferred_element_type=jnp.float32)

        return one(a_high, b_high) + (one(a_high, b_low) + one(a_low, b_high))

    points = land[...]
    inner = dots(high_ref[...], low_ref[...], *split(points))
    squares = square_ref[...] + jnp.sum(points * points, axis=0, keepdims=True)
    tile = jnp.exp(-2.0 * (squares - 2.0 * inner) / features)
    out[...] = tile
    pred[...] += dots(*split(tile), *split(current[...]))


def kernel_of(proj, land, current):
    rows, features = proj.shape
    length = land.shape[1]
    width = current.shape[1]
    step = min(512, length)
    return pl.pallas_call(
        kernel_kernel,
        grid=(length // step,),
        out_shape=(
            jax.ShapeDtypeStruct((rows, length), jnp.float32),
            jax.ShapeDtypeStruct((rows, width), jnp.float32),
        ),
        in_specs=[
            pl.BlockSpec((rows, features), lambda i: (0, 0)),
            pl.BlockSpec((features, step), lambda i: (0, i)),
            pl.BlockSpec((step, width), lambda i: (i, 0)),
        ],
        out_specs=(
            pl.BlockSpec((rows, step), lambda i: (0, i)),
            pl.BlockSpec((rows, width), lambda i: (0, 0)),
        ),
        scratch_shapes=[
            pltpu.VMEM((rows, features), jnp.bfloat16),
            pltpu.VMEM((rows, features), jnp.bfloat16),
            pltpu.VMEM((rows, 1), jnp.float32),
        ],
        cost_estimate=pl.CostEstimate(
            flops=6 * rows * length * (features + width),
            bytes_accessed=4 * length * (rows + features),
            transcendentals=rows * length,
        ),
        name="kernel",
    )(proj, land, current)


def on_device(documents, projection, landmarks, coefficients, inverse_tiles, labels):
    high = lax.Precision.HIGH
    rows, cols = lax.axis_size("row"), lax.axis_size("col")
    land_t, docs_t, proj_full = gather(rows, cols, landmarks.T, documents.T, projection)
    land_t = land_t.reshape(-1, land_t.shape[2])
    docs_t = docs_t.reshape(-1, docs_t.shape[2])
    proj_full = proj_full.reshape(-1, proj_full.shape[2])

    def dot(a, b, over_a, over_b):
        return lax.dot_general(
            a, b, (((over_a,), (over_b,)), ((), ())), precision=high, preferred_element_type=jnp.float32
        )

    kernel, predicted = kernel_of(dot(docs_t, proj_full, 0, 0), land_t, coefficients)
    step_size = 64.0 / (documents.shape[0] * rows)
    current = coefficients
    residual = None
    for iteration in range(ITERS):
        first_id = 1 + 3 * iteration
        if iteration > 0:
            predicted = dot(kernel, current, 1, 0)
        residual = residual_of(cols, predicted, labels, first_id)
        gradient = gradient_of(rows, cols, dot(kernel, residual, 0, 0), first_id + 1)
        product = product_of(inverse_tiles, gradient)
        current = update_of(rows, step_size, product, current, first_id + 2)
    return current, residual


def solution(mesh):
    in_specs = (
        P("row", "col"),
        P("col", None),
        P("col", "row"),
        P("col", None),
        P("col", "row"),
        P("row", None),
    )
    out_specs = (P("col", None), P("row", None))
    return jax.shard_map(
        on_device, mesh=mesh, in_specs=in_specs, out_specs=out_specs, check_vma=False
    )
```
